512 devices in a mesh: gx: 32 (over z, y_lo), gy: 16 (over y_hi, x, core).
Axes of the slice: x: 4, y: 4 (y_hi: 2, y_lo: 2; y = y_hi * 2 + y_lo), z: 16, core: 2. Of those that a mesh axis runs over, the one named last changes fastest.
Arguments:
- fields: float32 [5, 4, 1024, 2048], P(None, None, 'gx', 'gy'), may hold values from -6 to 6
- viscosity: float32 [4, 1024, 2048], P(None, 'gx', 'gy'), may hold values from 0.03 to 0.3
- precursor: float32 [5, 4, 512], P(None, None, 'gy'), may hold values from -6 to 6
- tile_index: int32 [2048], P('gy'), may hold values from 0 to 511, as said below
- fine_fields: float32 [8192, 5, 4, 4, 256], P(('gx', 'gy')), may hold values from -6 to 6
- fine_viscosity: float32 [8192, 4, 4, 256], P(('gx', 'gy')), may hold values from 0.03 to 0.3
- partner_gx: int32 [8192], P(('gx', 'gy')), may hold values from 0 to 31, as said below
- partner_col: int32 [8192], P(('gx', 'gy')), may hold values from 0 to 31
Outputs:
- fields_out: float32 [5, 4, 1024, 2048], P(None, None, 'gx', 'gy')
- fine_out: float32 [8192, 5, 4, 4, 256], P(('gx', 'gy'))
The draws below stay inside these ranges and needn't reach their ends.
Inputs may be any that keep to these rules, and one draw needn't show every extreme that they name: `tile_index`: inlet cell y takes precursor cell (y + s) mod 512, where s is drawn for each aligned block of 128 cells. `partner_gx`: each device's tiles are glued to outer devices of its own gy row: exactly 2 tiles to each of 8 distinct gx indices; in every gy row one gx index receives 2 tiles from every device of the row.
All inputs are finite; a program needn't handle non-finite values.
Results may differ from the reference program's by a relative error of at most 0.00005.
Values sent between devices are 32-bit elements; how exact they have to be, the bound alone decides.
No kernel may reach another device: no remote copies, remote signals or barrier semaphores. Data moves between devices by JAX's collectives and lax.ppermute only.
A program may use at most 64 MiB of HBM per device.

```python
import math
import jax
import jax.numpy as jnp
from jax import lax

F = 5
Z = 4
CX = 32
CY = 128
RX = 4
PW = 512
CAP = 2
RT_DEV = 16
NR = 8192
NX = 1024
NY = 2048
RW = 256
N_GX = 32
N_GY = 16


def draw_tile_index(key, part):
    shifts = jax.random.randint(jax.random.fold_in(key, 11), (NY // CY,), 0, PW)
    positions = jnp.arange(NY, dtype=jnp.int32)
    return ((positions + shifts[positions // CY]) % PW).astype(jnp.int32)


def draw_partner_gx(key, part):
    hot_target = jax.random.randint(jax.random.fold_in(key, 21), (N_GY,), 0, N_GX)
    shift_draw = jax.random.randint(jax.random.fold_in(key, 22), (N_GX, N_GY), 0, N_GX - 1)
    group_of = jnp.arange(RT_DEV, dtype=jnp.int32) // CAP
    other_target = (hot_target[None, :, None] + 1 + (group_of[None, None, :] - 1 + shift_draw[:, :, None]) % (N_GX - 1)) % N_GX
    targets = jnp.where(group_of[None, None, :] == 0, hot_target[None, :, None], other_target)
    targets = targets.reshape(N_GX * N_GY, RT_DEV)
    device_keys = jax.random.split(jax.random.fold_in(key, 23), N_GX * N_GY)
    shuffles = jax.vmap(lambda subkey: jax.random.permutation(subkey, RT_DEV))(device_keys)
    mixed = jnp.take_along_axis(targets, shuffles, axis=1)
    return mixed.reshape(NR).astype(jnp.int32)


def place_ends(array, key, least, high):
    shape = array.shape
    index_at = [jax.random.randint(jax.random.fold_in(key, axis), (), 0, shape[axis]) for axis in range(len(shape))]
    array = array.at[tuple(index_at)].set(least)
    longest = shape.index(max(shape))
    index_at[longest] = (index_at[longest] + 1) % shape[longest]
    return array.at[tuple(index_at)].set(high)


def steps_of(stream_key, shape, shards, smallest, top_value):
    loudness, own = 1.0, jax.random.fold_in(stream_key, 6)
    for axis_at, parts in shards:
        heights = jnp.exp(jax.random.uniform(jax.random.fold_in(own, axis_at), (parts,), jnp.float32, smallest / len(shards), top_value / len(shards)))
        loudness = loudness * jnp.repeat(heights, shape[axis_at] // parts).reshape([-1 if axis == axis_at else 1 for axis in range(len(shape))])
    return loudness


def noise(own_key, shape, scale, reach, pieces=(), kind=jnp.bfloat16):
    values = scale * jax.random.normal(own_key, shape, jnp.float32)
    if pieces:
        values = values * steps_of(own_key, shape, pieces, -0.22, 0.18)
    return jnp.clip(values, -reach, reach).astype(kind)


def setup_inputs(seed: int = 0) -> dict:
    arg_keys = jax.random.split(jax.random.key(seed), 9)
    fields = noise(arg_keys[0], (F, Z, NX, NY), 1.0, 6.0, ((2, 32), (3, 16)), jnp.float32)
    viscosity = jnp.clip(jnp.exp(math.log(0.3) - 2.3025852 * jax.random.uniform(arg_keys[1], (Z, NX, NY), jnp.float32) ** steps_of(arg_keys[1], (Z, NX, NY), ((1, 32), (2, 16)), -0.2, 0.2)), 0.03, 0.3)
    precursor = noise(arg_keys[2], (F, Z, PW), 1.0, 6.0, ((2, 16),), jnp.float32)
    tile_index = draw_tile_index(jax.random.fold_in(arg_keys[8], 71), 0)
    fine_fields = noise(arg_keys[4], (NR, F, Z, RX, RW), 1.0, 6.0, ((0, 512),), jnp.float32)
    fine_viscosity = jnp.clip(jnp.exp(math.log(0.3) - 2.3025852 * jax.random.uniform(arg_keys[5], (NR, Z, RX, RW), jnp.float32) ** steps_of(arg_keys[5], (NR, Z, RX, RW), ((0, 512),), -0.2, 0.2)), 0.03, 0.3)
    partner_gx = draw_partner_gx(jax.random.fold_in(arg_keys[8], 71), 0)
    partner_col = place_ends(jax.random.randint(arg_keys[7], (NR,), 0, CX), jax.random.fold_in(arg_keys[7], 1), 0, CX - 1).astype(jnp.int32)
    return dict(fields=fields, viscosity=viscosity, precursor=precursor, tile_index=tile_index, fine_fields=fine_fields, fine_viscosity=fine_viscosity, partner_gx=partner_gx, partner_col=partner_col)


time_step = 0.2
vertical_mix = 0.1
coarse_penalty = 0.5
fine_penalty = 1.0


def tendency(padded, spacing):
    nfield = padded.shape[-4] - 1
    state_part = padded[..., :nfield, :, :, :]
    visc_part = padded[..., nfield:, :, :, :]
    centre = state_part[..., 1:-1, 1:-1]
    q_east = state_part[..., 2:, 1:-1]
    q_west = state_part[..., :-2, 1:-1]
    q_north = state_part[..., 1:-1, 2:]
    q_south = state_part[..., 1:-1, :-2]
    u_flow = centre[..., 0:1, :, :, :]
    v_flow = centre[..., 1:2, :, :, :]
    nu_mid = visc_part[..., 1:-1, 1:-1]
    nu_east = 0.5 * (nu_mid + visc_part[..., 2:, 1:-1])
    nu_west = 0.5 * (nu_mid + visc_part[..., :-2, 1:-1])
    nu_north = 0.5 * (nu_mid + visc_part[..., 1:-1, 2:])
    nu_south = 0.5 * (nu_mid + visc_part[..., 1:-1, :-2])
    advect = (u_flow * (q_east - q_west) + v_flow * (q_north - q_south)) / (2.0 * spacing)
    diffuse = (nu_east * (q_east - centre) - nu_west * (centre - q_west)
               + nu_north * (q_north - centre) - nu_south * (centre - q_south)) / (spacing * spacing)
    q_above = jnp.concatenate([centre[..., 1:, :, :], centre[..., -1:, :, :]], axis=-3)
    q_below = jnp.concatenate([centre[..., :1, :, :], centre[..., :-1, :, :]], axis=-3)
    return diffuse - advect + vertical_mix * (q_above - 2.0 * centre + q_below)


def coarsen(trace_in):
    even_cells = trace_in[..., 0::2]
    odd_cells = trace_in[..., 1::2]
    left_cells = jnp.concatenate([trace_in[..., :1], odd_cells[..., :-1]], axis=-1)
    return 0.25 * left_cells + 0.5 * even_cells + 0.25 * odd_cells


def refine(trace_in):
    shifted = jnp.concatenate([trace_in[..., 1:], trace_in[..., -1:]], axis=-1)
    odd_cells = 0.5 * (trace_in + shifted)
    joined = jnp.stack([trace_in, odd_cells], axis=-1)
    return joined.reshape(trace_in.shape[:-1] + (2 * trace_in.shape[-1],))


def reference(fields, viscosity, precursor, tile_index, fine_fields, fine_viscosity, partner_gx, partner_col):
    inflow = precursor[:, :, tile_index]
    stacked = jnp.concatenate([fields, viscosity[None]], axis=0)
    inlet_ghost = jnp.concatenate([inflow, viscosity[None, :, 0, :]], axis=0)
    xpadded = jnp.concatenate([inlet_ghost[:, :, None, :], stacked, stacked[:, :, -1:, :]], axis=2)
    padded = jnp.concatenate([xpadded[..., -1:], xpadded, xpadded[..., :1]], axis=3)
    coarse_rate = tendency(padded, 1.0)

    fine_stack = jnp.concatenate([fine_fields, fine_viscosity[:, None]], axis=1)
    blocks = fine_stack.reshape((N_GX * N_GY, RT_DEV) + fine_stack.shape[1:])

    def block_rate(one_block):
        widened = jnp.pad(one_block, ((0, 0), (0, 0), (0, 0), (1, 1), (1, 1)), mode="edge")
        return tendency(widened, 0.5)

    fine_rate = lax.map(block_rate, blocks).reshape(fine_fields.shape)

    tile_ids = jnp.arange(NR, dtype=jnp.int32)
    row_of = (tile_ids // RT_DEV) % N_GY
    column = (partner_gx * CX + partner_col).astype(jnp.int32)
    span_cells = (row_of[:, None] * CY + jnp.arange(CY, dtype=jnp.int32)[None, :]).astype(jnp.int32)
    coarse_trace = jnp.transpose(fields[:, :, column[:, None], span_cells], (2, 0, 1, 3))
    fine_trace = fine_fields[:, :, :, 0, :]
    mismatch = coarse_penalty * (coarsen(fine_trace) - coarse_trace)
    coarse_sat = jnp.zeros_like(fields).at[:, :, column[:, None], span_cells].add(jnp.transpose(mismatch, (1, 2, 0, 3)))
    fields_out = fields + time_step * (coarse_rate + coarse_sat)
    fine_sat = fine_penalty * (refine(coarse_trace) - fine_trace)
    total_rate = fine_rate.at[:, :, :, 0, :].add(fine_sat)
    fine_out = fine_fields + time_step * total_rate
    return fields_out, fine_out
```

```python
import jax
import jax.numpy as jnp
from jax import lax
from jax.experimental import pallas as pl
from jax.experimental.pallas import tpu as pltpu
from jax.sharding import PartitionSpec as P


CAP = 2
VMEM_BYTES = 16 * 2**20
HIGHEST = lax.Precision.HIGHEST


time_step = 0.2
vertical_mix = 0.1
coarse_penalty = 0.5
fine_penalty = 1.0

WHOLE = pl.BlockSpec(memory_space=pltpu.VMEM)
SCALARS = pl.BlockSpec(memory_space=pltpu.SMEM)


def cost(flops, *arrays):
    return pl.CostEstimate(
        flops=flops, transcendentals=0, bytes_accessed=sum(4 * a.size for a in arrays)
    )


def coarsen_weights(width):
    fine = lax.broadcasted_iota(jnp.int32, (width, width // 2), 0)
    middle = 2 * lax.broadcasted_iota(jnp.int32, (width, width // 2), 1)
    sides = (fine == middle + 1) | (fine == middle - 1)
    weights = jnp.where(fine == middle, 0.5, jnp.where(sides, 0.25, 0.0))
    return weights + jnp.where((fine == 0) & (middle == 0), 0.25, 0.0)


def refine_weights(count):
    coarse = lax.broadcasted_iota(jnp.int32, (count, 2 * count), 0)
    fine = lax.broadcasted_iota(jnp.int32, (count, 2 * count), 1)
    lower = fine // 2
    upper = jnp.minimum((fine + 1) // 2, count - 1)
    return jnp.where(coarse == lower, 0.5, 0.0) + jnp.where(coarse == upper, 0.5, 0.0)


def ring_shift(cells, axis, step):
    count = lax.axis_size(axis)
    return lax.ppermute(cells, axis, [(i, (i + step) % count) for i in range(count)])


def pack_kernel(gx_ref, fine_ref, out_ref, slot_ref, seen_ref):
    groups = seen_ref.shape[0]
    tiles, nfield, levels, _, width = fine_ref.shape

    def clear(group, carry):
        seen_ref[group] = 0
        return carry

    lax.fori_loop(0, groups, clear, 0)
    out_ref[...] = jnp.zeros_like(out_ref)
    trace = fine_ref[:, :, :, 0, :].reshape(tiles * nfield * levels, width)
    cells = jnp.dot(
        trace, coarsen_weights(width), precision=HIGHEST, preferred_element_type=jnp.float32
    ).reshape(tiles, nfield, levels, width // 2)
    for i in range(tiles):
        target = gx_ref[i]
        slot = target * CAP + seen_ref[target]
        seen_ref[target] = seen_ref[target] + 1
        slot_ref[i] = slot
        out_ref[slot] = cells[i]


def pack_traces(partner_gx, fine_fields, groups):
    tiles, nfield, levels, _, width = fine_fields.shape
    sent = jax.ShapeDtypeStruct((groups * CAP, nfield, levels, width // 2), jnp.float32)
    return pl.pallas_call(
        pack_kernel,
        out_shape=(sent, jax.ShapeDtypeStruct((tiles,), jnp.int32)),
        in_specs=[SCALARS, WHOLE],
        out_specs=(WHOLE, SCALARS),
        scratch_shapes=[pltpu.SMEM((groups,), jnp.int32)],
        cost_estimate=cost(10**8, fine_fields, sent),
        compiler_params=pltpu.CompilerParams(vmem_limit_bytes=VMEM_BYTES),
        name="pack_traces",
    )(partner_gx, fine_fields)


def finish_kernel(slot_ref, back_ref, part_ref, out_ref, stage_ref, sems):
    step = pl.program_id(0)
    tiles, nfield, levels, _, width = part_ref.shape
    total = stage_ref.shape[0]

    def fetch(tile):
        return pltpu.make_async_copy(
            back_ref.at[slot_ref[tile]], stage_ref.at[tile], sems.at[tile]
        )

    @pl.when(step == 0)
    def _():
        for tile in range(total):
            fetch(tile).start()

    for i in range(tiles):
        fetch(step * tiles + i).wait()
    cells = stage_ref[pl.ds(step * tiles, tiles)].reshape(tiles * nfield * levels, width // 2)
    fine = jnp.dot(
        cells, refine_weights(width // 2), precision=HIGHEST, preferred_element_type=jnp.float32
    ).reshape(tiles, nfield, levels, width)
    out_ref[...] = part_ref[...]
    out_ref[:, :, :, 0, :] = part_ref[:, :, :, 0, :] + (time_step * fine_penalty) * fine


def finish_tiles(slots, back, part, block=4):
    tiles, nfield, levels, rows, width = part.shape
    spec = pl.BlockSpec((block, nfield, levels, rows, width), lambda i: (i, 0, 0, 0, 0))
    return pl.pallas_call(
        finish_kernel,
        grid=(tiles // block,),
        out_shape=jax.ShapeDtypeStruct(part.shape, jnp.float32),
        in_specs=[SCALARS, pl.BlockSpec(memory_space=pl.ANY), spec],
        out_specs=spec,
        scratch_shapes=[
            pltpu.VMEM((tiles, nfield, levels, width // 2), jnp.float32),
            pltpu.SemaphoreType.DMA((tiles,)),
        ],
        cost_estimate=cost(10**8, part, part, back),
        compiler_params=pltpu.CompilerParams(vmem_limit_bytes=VMEM_BYTES),
        name="finish_tiles",
    )(slots, back, part)


def neighbour(cells, axis, step):
    count = cells.shape[axis]
    if step > 0:
        parts = [(1, count), (count - 1, count)]
    else:
        parts = [(0, 1), (0, count - 1)]
    return jnp.concatenate([lax.slice_in_dim(cells, *p, axis=axis) for p in parts], axis=axis)


def fine_kernel(q_ref, nu_ref, out_ref):
    def one_tile(tile, carry):
        nu = nu_ref[tile]
        nu_east = 2.0 * (nu + neighbour(nu, 1, 1))
        nu_west = 2.0 * (nu + neighbour(nu, 1, -1))
        nu_north = 2.0 * (nu + neighbour(nu, 2, 1))
        nu_south = 2.0 * (nu + neighbour(nu, 2, -1))
        u_flow = q_ref[tile, 0]
        v_flow = q_ref[tile, 1]
        glued = lax.broadcasted_iota(jnp.int32, nu.shape, 1) == 0
        for field in range(q_ref.shape[1]):
            q = q_ref[tile, field]
            east, west = neighbour(q, 1, 1), neighbour(q, 1, -1)
            north, south = neighbour(q, 2, 1), neighbour(q, 2, -1)
            above, below = neighbour(q, 0, 1), neighbour(q, 0, -1)
            diffuse = (
                nu_east * (east - q)
                - nu_west * (q - west)
                + nu_north * (north - q)
                - nu_south * (q - south)
            )
            advect = u_flow * (east - west) + v_flow * (north - south)
            rate = diffuse - advect + vertical_mix * (above - 2.0 * q + below)
            out_ref[tile, field] = q + time_step * (
                rate - jnp.where(glued, fine_penalty * q, 0.0)
            )
        return carry

    lax.fori_loop(0, q_ref.shape[0], one_tile, 0)


def fine_step(fine_fields, fine_viscosity, block=4):
    tiles, nfield, levels, rows, width = fine_fields.shape
    spec = pl.BlockSpec((block, nfield, levels, rows, width), lambda i: (i, 0, 0, 0, 0))
    return pl.pallas_call(
        fine_kernel,
        grid=(tiles // block,),
        out_shape=jax.ShapeDtypeStruct(fine_fields.shape, jnp.float32),
        in_specs=[spec, pl.BlockSpec((block, levels, rows, width), lambda i: (i, 0, 0, 0))],
        out_specs=spec,
        cost_estimate=cost(10**8, fine_fields, fine_fields, fine_viscosity),
        compiler_params=pltpu.CompilerParams(vmem_limit_bytes=VMEM_BYTES),
        name="fine_step",
    )(fine_fields, fine_viscosity)


def coarse_kernel(
    wanted_ref,
    q_ref,
    nu_ref,
    west_ref,
    east_ref,
    south_ref,
    north_ref,
    came_ref,
    sent_ref,
    out_ref,
    sat_ref,
):
    nfield, levels, columns, span = q_ref.shape
    lane = lax.broadcasted_iota(jnp.int32, (columns, span), 1)
    sat_ref[...] = jnp.zeros_like(sat_ref)

    def add_slot(slot, carry):
        column = wanted_ref[slot]

        @pl.when(column >= 0)
        def _():
            sat_ref[column] += came_ref[slot] - sent_ref[slot]

        return carry

    lax.fori_loop(0, came_ref.shape[0], add_slot, 0)

    def around(q, which, level):
        row = which * levels + level
        east = jnp.concatenate([q[1:], east_ref[row : row + 1, :]], axis=0)
        west = jnp.concatenate([west_ref[row : row + 1, :], q[:-1]], axis=0)
        north = jnp.where(
            lane == span - 1, north_ref[:, row : row + 1], pltpu.roll(q, span - 1, 1)
        )
        south = jnp.where(lane == 0, south_ref[:, row : row + 1], pltpu.roll(q, 1, 1))
        return east, west, north, south

    for level in range(levels):
        nu = nu_ref[level]
        nu_east, nu_west, nu_north, nu_south = (
            0.5 * (nu + other) for other in around(nu, nfield, level)
        )
        u_flow = q_ref[0, level]
        v_flow = q_ref[1, level]
        for field in range(nfield):
            q = q_ref[field, level]
            east, west, north, south = around(q, field, level)
            above = q_ref[field, min(level + 1, levels - 1)]
            below = q_ref[field, max(level - 1, 0)]
            diffuse = (
                nu_east * (east - q)
                - nu_west * (q - west)
                + nu_north * (north - q)
                - nu_south * (q - south)
            )
            advect = 0.5 * (u_flow * (east - west) + v_flow * (north - south))
            rate = diffuse - advect + vertical_mix * (above - 2.0 * q + below)
            sat = coarse_penalty * sat_ref[:, field, level, :]
            out_ref[field, level] = q + time_step * (rate + sat)


def coarse_step(wanted, fields, viscosity, west, east, south, north, came, sent):
    nfield, levels, columns, span = fields.shape
    return pl.pallas_call(
        coarse_kernel,
        out_shape=jax.ShapeDtypeStruct(fields.shape, jnp.float32),
        in_specs=[SCALARS] + [WHOLE] * 8,
        out_specs=WHOLE,
        scratch_shapes=[pltpu.VMEM((columns, nfield, levels, span), jnp.float32)],
        cost_estimate=cost(10**8, fields, fields, came),
        compiler_params=pltpu.CompilerParams(vmem_limit_bytes=VMEM_BYTES),
        name="coarse_step",
    )(wanted, fields, viscosity, west, east, south, north, came, sent)


def on_device(
    fields, viscosity, precursor, tile_index, fine_fields, fine_viscosity, partner_gx, partner_col
):
    nfield, levels, columns, span_cells = fields.shape
    tiles = partner_gx.shape[0]
    groups = lax.axis_size("gx")
    my_gx = lax.axis_index("gx")
    my_gy = lax.axis_index("gy")
    block = (groups, CAP, nfield, levels, span_cells)

    sending, slots = pack_traces(partner_gx, fine_fields, groups)
    trace_in = lax.all_to_all(sending.reshape(block), "gx", split_axis=0, concat_axis=0, tiled=True)

    rows = jnp.concatenate([fields, viscosity[None]], axis=0)
    halo = (nfield + 1) * levels
    request = jnp.concatenate([partner_gx, partner_col]).astype(jnp.float32)[None, :]
    request = jnp.pad(request, ((0, 0), (0, span_cells - 2 * tiles)))
    low_row = rows[:, :, 0, :].reshape(halo, span_cells)
    high_row = rows[:, :, -1, :].reshape(halo, span_cells)
    from_west = ring_shift(jnp.concatenate([high_row, request], axis=0), "gx", 1)
    from_east = ring_shift(low_row, "gx", -1)
    asked = jnp.concatenate([request, from_west[halo:]], axis=0)
    while asked.shape[0] < groups:
        asked = jnp.concatenate([asked, ring_shift(asked, "gx", asked.shape[0])], axis=0)
    order = (
        jnp.arange(groups)[None, :] == (my_gx - jnp.arange(groups)[:, None]) % groups
    ).astype(jnp.float32)
    asked = jnp.einsum("sj,jc->sc", order, asked[:, : 2 * tiles], precision=HIGHEST)
    mine = asked[:, :tiles] == my_gx.astype(jnp.float32)
    earlier = jnp.arange(tiles)[None, :] < jnp.arange(tiles)[:, None]
    before = jnp.sum(jnp.where(earlier, mine[:, None, :], False).astype(jnp.int32), axis=2)
    wanted = []
    for rank in range(CAP):
        chosen = mine & (before == rank)
        wanted.append(jnp.sum(jnp.where(chosen, asked[:, tiles:] + 1.0, 0.0), axis=1) - 1.0)
    wanted = jnp.stack(wanted, axis=1)
    column_in = (wanted[:, :, None] == jnp.arange(columns, dtype=jnp.float32)).astype(jnp.float32)
    answer = jnp.einsum("gsx,fzxy->gsfzy", column_in, fields, precision=HIGHEST)
    returned = lax.all_to_all(answer, "gx", split_axis=0, concat_axis=0, tiled=True)

    low_col = rows[:, :, :, 0].reshape(halo, columns)
    high_col = rows[:, :, :, -1].reshape(halo, columns)
    width = precursor.shape[2]
    shard = precursor.reshape(nfield * levels, width)
    from_south = ring_shift(jnp.concatenate([high_col, shard], axis=0), "gy", 1)
    from_north = ring_shift(low_col, "gy", -1)
    shards = jnp.stack([shard, from_south[halo:]])
    count = lax.axis_size("gy")
    while shards.shape[0] < count:
        shards = jnp.concatenate([shards, ring_shift(shards, "gy", shards.shape[0])], axis=0)
    position = ((my_gy - tile_index // width) % count) * width + tile_index % width
    choose = (position[:, None] == jnp.arange(count * width)[None, :]).astype(jnp.float32)
    inflow = jnp.einsum(
        "jro,yjo->ry", shards, choose.reshape(-1, count, width), precision=HIGHEST
    )

    inlet = jnp.concatenate([inflow, viscosity[:, 0, :]], axis=0)
    west = jnp.where(my_gx == 0, inlet, from_west[:halo])
    east = jnp.where(my_gx == groups - 1, high_row, from_east)
    slab = (groups * CAP,) + block[2:]
    fields_out = coarse_step(
        wanted.reshape(groups * CAP).astype(jnp.int32),
        fields,
        viscosity,
        west,
        east,
        from_south[:halo].T,
        from_north.T,
        trace_in.reshape(slab),
        answer.reshape(slab),
    )

    part = fine_step(fine_fields, fine_viscosity)
    fine_out = finish_tiles(slots, returned.reshape(slab), part)
    return (fields_out, fine_out)


def solution(mesh):
    return jax.shard_map(
        on_device,
        mesh=mesh,
        in_specs=(
            P(None, None, "gx", "gy"),
            P(None, "gx", "gy"),
            P(None, None, "gy"),
            P("gy"),
            P(("gx", "gy"), None, None, None, None),
            P(("gx", "gy"), None, None, None),
            P(("gx", "gy")),
            P(("gx", "gy")),
        ),
        out_specs=(P(None, None, "gx", "gy"), P(("gx", "gy"), None, None, None, None)),
        check_vma=False,
    )
```

```python
import jax
import jax.numpy as jnp
from jax import lax
from jax.experimental import pallas as pl
from jax.experimental.pallas import tpu as pltpu
from jax.sharding import PartitionSpec as P


CAP = 2
VMEM_BYTES = 16 * 2**20
HIGHEST = lax.Precision.HIGHEST


time_step = 0.2
vertical_mix = 0.1
coarse_penalty = 0.5
fine_penalty = 1.0

WHOLE = pl.BlockSpec(memory_space=pltpu.VMEM)
SCALARS = pl.BlockSpec(memory_space=pltpu.SMEM)


def cost(flops, *arrays):
    return pl.CostEstimate(
        flops=flops, transcendentals=0, bytes_accessed=sum(4 * a.size for a in arrays)
    )


def coarsen_weights(width):
    fine = lax.broadcasted_iota(jnp.int32, (width, width // 2), 0)
    middle = 2 * lax.broadcasted_iota(jnp.int32, (width, width // 2), 1)
    sides = (fine == middle + 1) | (fine == middle - 1)
    weights = jnp.where(fine == middle, 0.5, jnp.where(sides, 0.25, 0.0))
    return weights + jnp.where((fine == 0) & (middle == 0), 0.25, 0.0)


def refine_weights(count):
    coarse = lax.broadcasted_iota(jnp.int32, (count, 2 * count), 0)
    fine = lax.broadcasted_iota(jnp.int32, (count, 2 * count), 1)
    lower = fine // 2
    upper = jnp.minimum((fine + 1) // 2, count - 1)
    return jnp.where(coarse == lower, 0.5, 0.0) + jnp.where(coarse == upper, 0.5, 0.0)


def ring_shift(cells, axis, step):
    count = lax.axis_size(axis)
    return lax.ppermute(cells, axis, [(i, (i + step) % count) for i in range(count)])


def pack_kernel(gx_ref, col_ref, fine_ref, out_ref, slot_ref, trace_ref, seen_ref, sems):
    groups, rows = out_ref.shape[:2]
    tiles, nfield, levels, width = trace_ref.shape
    slab = (rows - 1) // CAP
    chunk = tiles // sems.shape[0]

    def fetch(part):
        some = pl.ds(part * chunk, chunk)
        return pltpu.make_async_copy(
            fine_ref.at[some, :, :, 0, :], trace_ref.at[some], sems.at[part]
        )

    for part in range(tiles // chunk):
        fetch(part).start()

    def clear(group, carry):
        seen_ref[group] = 0
        return carry

    lax.fori_loop(0, groups, clear, 0)
    out_ref[:, : rows - 1] = jnp.zeros((groups, rows - 1) + out_ref.shape[2:], jnp.float32)
    out_ref[:, rows - 1] = jnp.full((groups,) + out_ref.shape[2:], -1.0, jnp.float32)
    weights = coarsen_weights(width)
    lane = lax.broadcasted_iota(jnp.int32, out_ref.shape[2:], 1)
    for part in range(tiles // chunk):
        fetch(part).wait()
        trace = trace_ref[pl.ds(part * chunk, chunk)].reshape(chunk * nfield * levels, width)
        cells = jnp.dot(
            trace, weights, precision=HIGHEST, preferred_element_type=jnp.float32
        ).reshape((chunk, slab) + out_ref.shape[2:])
        for i in range(chunk):
            tile = part * chunk + i
            target = gx_ref[tile]
            rank = seen_ref[target]
            seen_ref[target] = rank + 1
            slot_ref[tile] = target * CAP + rank
            out_ref[target, pl.ds(rank * slab, slab)] = cells[i]
            column = jnp.full(lane.shape, col_ref[tile], jnp.int32).astype(jnp.float32)
            out_ref[target, rows - 1] = jnp.where(lane == rank, column, out_ref[target, rows - 1])


def pack_traces(partner_gx, partner_col, fine_fields, groups):
    tiles, nfield, levels, _, width = fine_fields.shape
    slab = nfield * levels // 2
    sent = jax.ShapeDtypeStruct((groups, CAP * slab + 1, 2, width // 2), jnp.float32)
    return pl.pallas_call(
        pack_kernel,
        out_shape=(sent, jax.ShapeDtypeStruct((tiles,), jnp.int32)),
        in_specs=[SCALARS, SCALARS, pl.BlockSpec(memory_space=pl.ANY)],
        out_specs=(WHOLE, SCALARS),
        scratch_shapes=[
            pltpu.VMEM((tiles, nfield, levels, width), jnp.float32),
            pltpu.SMEM((groups,), jnp.int32),
            pltpu.SemaphoreType.DMA((4,)),
        ],
        cost_estimate=cost(10**8, fine_fields, sent),
        name="pack_traces",
    )(partner_gx, partner_col, fine_fields)


def answer_kernel(came_ref, q_ref, out_ref):
    nfield, levels, columns, _ = q_ref.shape
    groups, rows = came_ref.shape[:2]
    asked = came_ref[:, rows - 1, 0, :]
    column = lax.broadcasted_iota(jnp.int32, (groups, columns), 1).astype(jnp.float32)
    for rank in range(CAP):
        picked = jnp.where(asked[:, rank : rank + 1] == column, 1.0, 0.0)
        for row in range(nfield * levels):
            trace = jnp.dot(
                picked,
                q_ref[row // levels, row % levels],
                precision=HIGHEST,
                preferred_element_type=jnp.float32,
            )
            at = rank * nfield * levels + row
            out_ref[:, at // 2, at % 2, :] = trace


def answer_requests(came, fields):
    nfield, levels, _, span = fields.shape
    shape = (came.shape[0], CAP * nfield * levels // 2, 2, span)
    return pl.pallas_call(
        answer_kernel,
        out_shape=jax.ShapeDtypeStruct(shape, jnp.float32),
        in_specs=[WHOLE, WHOLE],
        out_specs=WHOLE,
        compiler_params=pltpu.CompilerParams(vmem_limit_bytes=VMEM_BYTES),
        cost_estimate=cost(10**8, came, fields),
        name="answer_requests",
    )(came, fields)


def finish_kernel(slot_ref, back_ref, part_ref, out_ref, stage_ref, sems):
    step = pl.program_id(0)
    tiles, nfield, levels, _, width = part_ref.shape
    total = stage_ref.shape[0]

    def fetch(tile):
        slot = slot_ref[tile]
        return pltpu.make_async_copy(
            back_ref.at[slot // CAP, pl.ds(slot % CAP * stage_ref.shape[1], stage_ref.shape[1])],
            stage_ref.at[tile],
            sems.at[tile],
        )

    @pl.when(step == 0)
    def _():
        for tile in range(total):
            fetch(tile).start()

    for i in range(tiles):
        fetch(step * tiles + i).wait()
    cells = stage_ref[pl.ds(step * tiles, tiles)].reshape(tiles * nfield * levels, width // 2)
    fine = jnp.dot(
        cells, refine_weights(width // 2), precision=HIGHEST, preferred_element_type=jnp.float32
    ).reshape(tiles, nfield, levels, width)
    out_ref[...] = part_ref[...]
    out_ref[:, :, :, 0, :] = part_ref[:, :, :, 0, :] + (time_step * fine_penalty) * fine


def finish_tiles(slots, back, part, block=4):
    tiles, nfield, levels, rows, width = part.shape
    spec = pl.BlockSpec((block, nfield, levels, rows, width), lambda i: (i, 0, 0, 0, 0))
    return pl.pallas_call(
        finish_kernel,
        grid=(tiles // block,),
        out_shape=jax.ShapeDtypeStruct(part.shape, jnp.float32),
        in_specs=[SCALARS, pl.BlockSpec(memory_space=pl.ANY), spec],
        out_specs=spec,
        scratch_shapes=[
            pltpu.VMEM((tiles, nfield * levels // 2, 2, width // 2), jnp.float32),
            pltpu.SemaphoreType.DMA((tiles,)),
        ],
        cost_estimate=cost(10**8, part, part, back),
        compiler_params=pltpu.CompilerParams(vmem_limit_bytes=VMEM_BYTES),
        name="finish_tiles",
    )(slots, back, part)


def neighbour(cells, axis, step):
    count = cells.shape[axis]
    if step > 0:
        parts = [(1, count), (count - 1, count)]
    else:
        parts = [(0, 1), (0, count - 1)]
    return jnp.concatenate([lax.slice_in_dim(cells, *p, axis=axis) for p in parts], axis=axis)


def fine_kernel(q_ref, nu_ref, out_ref):
    def one_tile(tile, carry):
        nu = nu_ref[tile]
        nu_east = 2.0 * (nu + neighbour(nu, 1, 1))
        nu_west = 2.0 * (nu + neighbour(nu, 1, -1))
        nu_north = 2.0 * (nu + neighbour(nu, 2, 1))
        nu_south = 2.0 * (nu + neighbour(nu, 2, -1))
        u_flow = q_ref[tile, 0]
        v_flow = q_ref[tile, 1]
        glued = lax.broadcasted_iota(jnp.int32, nu.shape, 1) == 0
        for field in range(q_ref.shape[1]):
            q = q_ref[tile, field]
            east, west = neighbour(q, 1, 1), neighbour(q, 1, -1)
            north, south = neighbour(q, 2, 1), neighbour(q, 2, -1)
            above, below = neighbour(q, 0, 1), neighbour(q, 0, -1)
            diffuse = (
                nu_east * (east - q)
                - nu_west * (q - west)
                + nu_north * (north - q)
                - nu_south * (q - south)
            )
            advect = u_flow * (east - west) + v_flow * (north - south)
            rate = diffuse - advect + vertical_mix * (above - 2.0 * q + below)
            out_ref[tile, field] = q + time_step * (
                rate - jnp.where(glued, fine_penalty * q, 0.0)
            )
        return carry

    lax.fori_loop(0, q_ref.shape[0], one_tile, 0)


def fine_step(fine_fields, fine_viscosity, block=4):
    tiles, nfield, levels, rows, width = fine_fields.shape
    spec = pl.BlockSpec((block, nfield, levels, rows, width), lambda i: (i, 0, 0, 0, 0))
    return pl.pallas_call(
        fine_kernel,
        grid=(tiles // block,),
        out_shape=jax.ShapeDtypeStruct(fine_fields.shape, jnp.float32),
        in_specs=[spec, pl.BlockSpec((block, levels, rows, width), lambda i: (i, 0, 0, 0))],
        out_specs=spec,
        cost_estimate=cost(10**8, fine_fields, fine_fields, fine_viscosity),
        compiler_params=pltpu.CompilerParams(vmem_limit_bytes=VMEM_BYTES),
        name="fine_step",
    )(fine_fields, fine_viscosity)


def coarse_kernel(
    wanted_ref,
    q_ref,
    nu_ref,
    west_ref,
    east_ref,
    south_ref,
    north_ref,
    came_ref,
    sent_ref,
    out_ref,
    sat_ref,
):
    nfield, levels, columns, span = q_ref.shape
    lane = lax.broadcasted_iota(jnp.int32, (columns, span), 1)
    sat_ref[...] = jnp.zeros_like(sat_ref)

    slab = sat_ref.shape[1]

    def add_slot(slot, carry):
        column = wanted_ref[slot]
        rows = pl.ds(slot % CAP * slab, slab)

        @pl.when(column >= 0)
        def _():
            sat_ref[column] += came_ref[slot // CAP, rows] - sent_ref[slot // CAP, rows]

        return carry

    lax.fori_loop(0, came_ref.shape[0] * CAP, add_slot, 0)

    def around(q, which, level):
        row = which * levels + level
        east = jnp.concatenate([q[1:], east_ref[row : row + 1, :]], axis=0)
        west = jnp.concatenate([west_ref[row : row + 1, :], q[:-1]], axis=0)
        north = jnp.where(
            lane == span - 1, north_ref[:, row : row + 1], pltpu.roll(q, span - 1, 1)
        )
        south = jnp.where(lane == 0, south_ref[:, row : row + 1], pltpu.roll(q, 1, 1))
        return east, west, north, south

    for level in range(levels):
        nu = nu_ref[level]
        nu_east, nu_west, nu_north, nu_south = (
            0.5 * (nu + other) for other in around(nu, nfield, level)
        )
        u_flow = q_ref[0, level]
        v_flow = q_ref[1, level]
        for field in range(nfield):
            q = q_ref[field, level]
            east, west, north, south = around(q, field, level)
            above = q_ref[field, min(level + 1, levels - 1)]
            below = q_ref[field, max(level - 1, 0)]
            diffuse = (
                nu_east * (east - q)
                - nu_west * (q - west)
                + nu_north * (north - q)
                - nu_south * (q - south)
            )
            advect = 0.5 * (u_flow * (east - west) + v_flow * (north - south))
            rate = diffuse - advect + vertical_mix * (above - 2.0 * q + below)
            sat = coarse_penalty * sat_ref[:, (field * levels + level) // 2, level % 2, :]
            out_ref[field, level] = q + time_step * (rate + sat)


def coarse_step(wanted, fields, viscosity, west, east, south, north, came, sent):
    nfield, levels, columns, span = fields.shape
    return pl.pallas_call(
        coarse_kernel,
        out_shape=jax.ShapeDtypeStruct(fields.shape, jnp.float32),
        in_specs=[SCALARS] + [WHOLE] * 8,
        out_specs=WHOLE,
        scratch_shapes=[pltpu.VMEM((columns, nfield * levels // 2, 2, span), jnp.float32)],
        cost_estimate=cost(10**8, fields, fields, came),
        compiler_params=pltpu.CompilerParams(vmem_limit_bytes=VMEM_BYTES),
        name="coarse_step",
    )(wanted, fields, viscosity, west, east, south, north, came, sent)


def on_device(
    fields, viscosity, precursor, tile_index, fine_fields, fine_viscosity, partner_gx, partner_col
):
    nfield, levels, columns, span_cells = fields.shape
    groups = lax.axis_size("gx")
    my_gx = lax.axis_index("gx")
    my_gy = lax.axis_index("gy")
    halo = (nfield + 1) * levels

    sending, slots = pack_traces(partner_gx, partner_col, fine_fields, groups)
    came = lax.all_to_all(sending, "gx", split_axis=0, concat_axis=0, tiled=True)
    sent = answer_requests(came, fields)
    returned = lax.all_to_all(sent, "gx", split_axis=0, concat_axis=0, tiled=True)
    wanted = came[:, -1, 0, :CAP].reshape(groups * CAP).astype(jnp.int32)

    rows = jnp.concatenate([fields, viscosity[None]], axis=0)
    low_row = rows[:, :, 0, :].reshape(halo, span_cells)
    high_row = rows[:, :, -1, :].reshape(halo, span_cells)
    from_west = ring_shift(high_row, "gx", 1)
    from_east = ring_shift(low_row, "gx", -1)
    low_col = rows[:, :, :, 0].reshape(halo, columns)
    high_col = rows[:, :, :, -1].reshape(halo, columns)
    width = precursor.shape[2]
    shard = precursor.reshape(nfield * levels, width)
    from_south = ring_shift(jnp.concatenate([high_col, shard], axis=0), "gy", 1)
    from_north = ring_shift(low_col, "gy", -1)
    count = lax.axis_size("gy")
    near = [shard, from_south[halo:]] + [ring_shift(shard, "gy", s) for s in (2, 3)]
    near = jnp.concatenate(near, axis=0)
    shards = [near] + [ring_shift(near, "gy", s) for s in range(4, count, 4)]
    shards = jnp.concatenate(shards, axis=0).reshape(-1, nfield * levels, width)
    position = ((my_gy - tile_index // width) % count) * width + tile_index % width
    choose = (position[:, None] == jnp.arange(shards.shape[0] * width)[None, :]).astype(jnp.float32)
    inflow = jnp.einsum(
        "jro,yjo->ry", shards, choose.reshape(-1, shards.shape[0], width), precision=HIGHEST
    )

    inlet = jnp.concatenate([inflow, viscosity[:, 0, :]], axis=0)
    west = jnp.where(my_gx == 0, inlet, from_west)
    east = jnp.where(my_gx == groups - 1, high_row, from_east)
    fields_out = coarse_step(
        wanted, fields, viscosity, west, east, from_south[:halo].T, from_north.T, came, sent
    )

    part = fine_step(fine_fields, fine_viscosity)
    fine_out = finish_tiles(slots, returned, part)
    return (fields_out, fine_out)


def solution(mesh):
    return jax.shard_map(
        on_device,
        mesh=mesh,
        in_specs=(
            P(None, None, "gx", "gy"),
            P(None, "gx", "gy"),
            P(None, None, "gy"),
            P("gy"),
            P(("gx", "gy"), None, None, None, None),
            P(("gx", "gy"), None, None, None),
            P(("gx", "gy")),
            P(("gx", "gy")),
        ),
        out_specs=(P(None, None, "gx", "gy"), P(("gx", "gy"), None, None, None, None)),
        check_vma=False,
    )
```
